256 devices in a mesh: blk: 64 (over y, x_lo, z), rep: 4 (over x_hi, core).
Axes of the slice: x: 4 (x_hi: 2, x_lo: 2; x = x_hi * 2 + x_lo), y: 4, z: 8, core: 2. Of those that a mesh axis runs over, the one named last changes fastest.
Arguments:
- tile_vals: bfloat16 [64, 8, 20, 128, 128], P('blk', 'rep'), may hold values from -4 to 4
- tile_coords: int32 [64, 8, 20, 2], P('blk', 'rep'), may hold values from 0 to 3
- tile_live: int32 [64, 8, 20], P('blk', 'rep'), may hold values from 0 to 1, as said below
- features: bfloat16 [32768, 256], P('blk'), may hold values from -6 to 6
- degree: int32 [32768], P(('blk', 'rep')), may hold values from 512 to 8192
- w_self: bfloat16 [256, 256], replicated, may hold values from -0.375 to 0.375
- w_neigh: bfloat16 [256, 256], replicated, may hold values from -0.375 to 0.375
- cotangent: bfloat16 [32768, 256], P(('blk', 'rep')), may hold values from -6 to 6
Outputs:
- hidden: bfloat16 [32768, 256], P(('blk', 'rep'))
- grad_features: bfloat16 [32768, 256], P(('blk', 'rep'))
- grad_self: float32 [256, 256], replicated
- grad_neigh: float32 [256, 256], replicated
The draws below stay inside these ranges and needn't reach their ends.
Inputs may be any that keep to these rules, and one draw needn't show every extreme that they name: `tile_coords`: entry 0 names a tile row block of the row partition, entry 1 a tile column block of the column partition; tiles with equal coordinates add. `tile_live`: 1 marks a present tile, 0 a padding tile; the share of present tiles differs between row partitions.
All inputs are finite; a program needn't handle non-finite values.
Results may differ from the reference program's by a relative error of at most 0.012.
Values may be sent and summed in bfloat16 or wider, within the bound.
A program may use at most 64 MiB of HBM per device.

```python
import math
import jax
import jax.numpy as jnp
from jax import lax

D = 256
TILE = 128
ROWS_DEV = 512
BLOCKS_DEV = 4
TILES = 20
PARTITIONS = 64
OFFS = 8
NODES = 32768


def draw_tile_live(key, part):
    rate_key = jax.random.fold_in(key, 17)
    coin_key = jax.random.fold_in(key, 29)
    rates = jax.random.randint(rate_key, (PARTITIONS, 1, 1), 2, 9)
    coins = jax.random.randint(coin_key, (PARTITIONS, OFFS, TILES), 0, 8)
    return (coins < rates).astype(jnp.int32)


def touch_ends(entries, stream_key, low, largest):
    place = [jax.random.randint(jax.random.fold_in(stream_key, axis), (), 0, length) for axis, length in enumerate(entries.shape)]
    longest = entries.shape.index(max(entries.shape))
    beside = place[:longest] + [(place[longest] + 1) % entries.shape[longest]] + place[longest + 1:]
    return entries.at[tuple(place)].set(low).at[tuple(beside)].set(largest)


def block_levels(stream_key, extent, shards, least, largest):
    def one(dim, shards_of):
        draws = jax.random.uniform(jax.random.fold_in(jax.random.fold_in(stream_key, 6), dim), (shards_of,), jnp.float32, least / len(shards), largest / len(shards))
        return jnp.repeat(jnp.exp(draws), extent[dim] // shards_of).reshape((-1,) + (1,) * (len(extent) - dim - 1))

    loudness = one(*shards[0])
    for cut in shards[1:]:
        loudness = loudness * one(*cut)
    return loudness


def centred(rng, extent, deviation, bound, cuts=(), kind=jnp.bfloat16):
    factor_of = block_levels(rng, extent, cuts, -0.22, 0.18) if cuts else 1.0
    drawn = jax.random.normal(rng, extent, jnp.float32) * deviation * factor_of
    return jnp.minimum(jnp.maximum(drawn, -bound), bound).astype(kind)


def setup_inputs(seed: int = 0) -> dict:
    seeds = jax.random.split(jax.random.key(seed), 9)
    return {
        "tile_vals": centred(seeds[0], (PARTITIONS, OFFS, TILES, TILE, TILE), 1.0, 4.0, ((0, 64), (1, 4))),
        "tile_coords": touch_ends(jax.random.randint(seeds[1], (PARTITIONS, OFFS, TILES, 2), 0, BLOCKS_DEV), jax.random.fold_in(seeds[1], 1), 0, BLOCKS_DEV - 1).astype(jnp.int32),
        "tile_live": draw_tile_live(jax.random.fold_in(seeds[8], 71), 0),
        "features": centred(seeds[3], (NODES, D), 1.0, 6.0, ((0, 64),)),
        "degree": touch_ends(jax.random.randint(seeds[4], (NODES,), 512, 8193), jax.random.fold_in(seeds[4], 1), 512, 8192).astype(jnp.int32),
        "w_self": centred(seeds[5], (D, D), D ** -0.5, 0.375),
        "w_neigh": centred(seeds[6], (D, D), D ** -0.5, 0.375),
        "cotangent": centred(seeds[7], (NODES, D), 1.0, 6.0, ((0, 256),)),
    }


def reference(tile_vals, tile_coords, tile_live, features, degree, w_self, w_neigh, cotangent):
    half_span = OFFS // 2
    offset_ids = jnp.arange(OFFS, dtype=jnp.int32)
    block_ids = jnp.arange(BLOCKS_DEV, dtype=jnp.int32)
    panels = features.reshape(PARTITIONS, BLOCKS_DEV, TILE, D)

    def forward_part(row_part):
        col_panels = (row_part + offset_ids - half_span) % PARTITIONS
        source_rows = panels[col_panels[:, None], tile_coords[row_part, :, :, 1]]
        tiles = tile_vals[row_part].astype(jnp.float32) * tile_live[row_part].astype(jnp.float32)[:, :, None, None]
        products = jnp.einsum('qkrc,qkcd->qkrd', tiles, source_rows.astype(jnp.float32))
        onehot = (tile_coords[row_part, :, :, 0][None] == block_ids[:, None, None]).astype(jnp.float32)
        placed = jnp.einsum('iqk,qkrd->ird', onehot, products, precision=lax.Precision.HIGHEST)
        return placed.reshape(ROWS_DEV, D)
    summed = lax.map(forward_part, jnp.arange(PARTITIONS, dtype=jnp.int32)).reshape(NODES, D)
    root_deg = jnp.sqrt(degree.astype(jnp.float32))[:, None]
    aggregate = (summed / root_deg).astype(jnp.bfloat16)
    preact = jnp.dot(features, w_self, preferred_element_type=jnp.float32) + jnp.dot(aggregate, w_neigh, preferred_element_type=jnp.float32)
    sigmoid_pre = jax.nn.sigmoid(preact)
    hidden = (preact * sigmoid_pre).astype(jnp.bfloat16)
    silu_slope = sigmoid_pre * (1.0 + preact * (1.0 - sigmoid_pre))
    grad_pre = (cotangent.astype(jnp.float32) * silu_slope).astype(jnp.bfloat16)
    grad_scale = 1.0 / math.sqrt(NODES)
    grad_self = jnp.dot(features.T, grad_pre, preferred_element_type=jnp.float32) * grad_scale
    grad_neigh = jnp.dot(aggregate.T, grad_pre, preferred_element_type=jnp.float32) * grad_scale
    back_proj = (jnp.dot(grad_pre, w_neigh.T, preferred_element_type=jnp.float32) / root_deg).astype(jnp.bfloat16)
    back_panels = back_proj.reshape(PARTITIONS, BLOCKS_DEV, TILE, D)
    own_term = jnp.dot(grad_pre, w_self.T, preferred_element_type=jnp.float32)

    def backward_part(col_part):
        sources = (col_part - offset_ids + half_span) % PARTITIONS
        tiles = tile_vals[sources, offset_ids].astype(jnp.float32) * tile_live[sources, offset_ids].astype(jnp.float32)[:, :, None, None]
        row_blocks = tile_coords[sources, offset_ids, :, 0]
        col_blocks = tile_coords[sources, offset_ids, :, 1]
        picked = back_panels[sources[:, None], row_blocks]
        products = jnp.einsum('qkrc,qkrd->qkcd', tiles, picked.astype(jnp.float32))
        onehot = (col_blocks[None] == block_ids[:, None, None]).astype(jnp.float32)
        placed = jnp.einsum('jqk,qkcd->jcd', onehot, products, precision=lax.Precision.HIGHEST)
        return placed.reshape(ROWS_DEV, D)
    neighbour = lax.map(backward_part, jnp.arange(PARTITIONS, dtype=jnp.int32)).reshape(NODES, D)
    grad_features = (own_term + neighbour).astype(jnp.bfloat16)
    return (hidden, grad_features, grad_self, grad_neigh)
```

```python
import functools
import math

import jax
import jax.numpy as jnp
from jax import lax
from jax.experimental import pallas as pl
from jax.experimental.pallas import tpu as pltpu
from jax.sharding import PartitionSpec as P

Y, X_LO, Z, X_HI = 4, 2, 8, 2
X = X_LO * X_HI
MESH = pl.DeviceIdType.MESH
F32, BF16 = jnp.float32, jnp.bfloat16


def flag(cond):
    return jnp.where(cond, 1, 0)


def layer_kernel(
    tiles_hbm, coords, live, feat_hbm, degree, w_self, w_neigh, cot,
    hidden, grad_feat, grad_self, grad_neigh,
    tiles, own, panels, dense, dense_t, pair_out, pair_in, chip_out, chip_in, back,
    wpair_out, wpair_in, wy_out, wy_in, wx_out, wx_in, wz_all, wgrad,
    terms, chain_out, chain_in, final_in,
    local_sem, feat_send, relay_send, feat_recv, rep_send, rep_recv, back_send, back_recv,
    wpair_sem, wy_send, wy_recv, wx_send, wx_recv, wz_send, wz_recv, ax_send, ax_recv, ay_send, ay_recv, ac_sem,
    chain_send, chain_recv, final_recv,
):
    blk_total = Y * X_LO * Z
    b, r = lax.axis_index("blk"), lax.axis_index("rep")
    z, x_lo, y = b % Z, (b // Z) % X_LO, b // (Z * X_LO)
    x_hi, core = r // 2, r % 2
    x = x_hi * X_LO + x_lo
    tile = tiles.shape[2]
    depth = own.shape[1]
    rows = panels.shape[1]
    blocks = rows // tile
    tile_count = tiles.shape[1]
    up = jnp.where(x_hi == 0, 1, blk_total - 1)
    b_up = (b + up) % blk_total
    b_down = (b + blk_total - up) % blk_total

    def y_peer(step):
        return (((y + step) % Y) * X_LO + x_lo) * Z + z, r

    def x_peer(step):
        at = (x + step) % X
        return (y * X_LO + at % X_LO) * Z + z, (at // X_LO) * 2 + core

    def z_peer(step):
        return (y * X_LO + x_lo) * Z + (z + step) % Z, r

    sibling = (b, r + 1 - 2 * core)
    across = (b, (r + 2) % 4)

    def remote(src, dst, send, recv, peer):
        return pltpu.make_async_remote_copy(
            src_ref=src, dst_ref=dst, send_sem=send, recv_sem=recv, device_id=peer, device_id_type=MESH
        )

    def arrived(dst, send, recv):
        remote(dst, dst, send, recv, sibling).wait_recv()

    def chunk(index, size=tile):
        return pl.ds(pl.multiple_of(index * size, size), size)

    tile_copy = pltpu.make_async_copy(tiles_hbm.at[0], tiles, local_sem.at[0])
    tile_copy.start()
    own_copy = pltpu.make_async_copy(feat_hbm.at[chunk(r)], own, local_sem.at[1])
    own_copy.start()

    panel_copy = pltpu.make_async_copy(feat_hbm, panels.at[0], local_sem.at[2])

    @pl.when(r == 2)
    def _():
        panel_copy.start()

    barrier = pltpu.get_barrier_semaphore()
    greeted = 0
    peers = [(b_next, (r + turn) % 4) for b_next in (b_up, b_down) for turn in range(4)]
    peers += [(b, (r + turn) % 4) for turn in range(1, 4)]
    peers += [y_peer(step) for step in range(1, Y)]
    peers += [x_peer(step) for step in range(1, X)]
    peers += [z_peer(step) for step in range(1, Z)]
    for peer in peers:
        pl.semaphore_signal(barrier, inc=1, device_id=peer, device_id_type=MESH)
        greeted += 1
    pl.semaphore_wait(barrier, greeted)

    first = (r == 1) | (r == 2)
    relay_slot = jnp.where(r == 3, 0, 1)
    relay_rep = jnp.where(r == 2, 3, r)

    def first_send(j):
        return remote(
            feat_hbm.at[chunk(j)], panels.at[1, chunk(j)], feat_send.at[j], feat_recv.at[1, j], (b_up, r)
        )

    def relay_a(j):
        return remote(
            panels.at[relay_slot, chunk(j)], panels.at[1 - relay_slot, chunk(j)],
            relay_send.at[0, j], feat_recv.at[1 - relay_slot, j], (b_up, relay_rep),
        )

    def relay_b(j):
        return remote(
            panels.at[0, chunk(j)], panels.at[1, chunk(j)], relay_send.at[1, j], feat_recv.at[1, j], (b_up, 0)
        )

    def panel_arrived(slot, j):
        arrived(panels.at[slot, chunk(j)], feat_send.at[j], feat_recv.at[slot, j])

    @pl.when(first)
    def _():
        @pl.loop(0, blocks)
        def _(j):
            first_send(j).start()

    tile_copy.wait()
    own_copy.wait()

    def build(slot, i):
        at = (i % 2) * 2 + i // 2

        @pl.loop(0, blocks)
        def _(j):
            total = jnp.zeros((tile, tile), F32)
            for k in range(tile_count):
                here = (coords[0, slot, k, 0] == i) & (coords[0, slot, k, 1] == j)
                weight = (flag(here) * live[0, slot, k]).astype(F32)
                total += tiles[slot, k].astype(F32) * weight
            dense[slot, chunk(at), chunk(j)] = total.astype(BF16)
            dense_t[slot, chunk(j), chunk(at)] = total.T.astype(BF16)

    @pl.loop(0, blocks)
    def _(j):
        build(0, j)
        panel_arrived(relay_slot, j)
        relay_a(j).start()

    @pl.loop(0, blocks)
    def _(j):
        build(1, j)

        @pl.when(r == 1)
        def _():
            panel_arrived(0, j)
            relay_b(j).start()

    own_rows = own[...]
    pre_self = jnp.dot(own_rows, w_self[...], preferred_element_type=F32)
    degrees = jnp.broadcast_to(degree[...].astype(F32), (tile, tile))
    root_half = jnp.sqrt(degrees.T)
    root = jnp.concatenate([root_half] * (depth // tile), axis=1)

    @pl.when(r == 2)
    def _():
        panel_copy.wait()

    @pl.when(r == 0)
    def _():
        @pl.loop(0, blocks)
        def _(j):
            panel_arrived(0, j)

    @pl.when((r == 2) | (r == 3))
    def _():
        @pl.when(r == 3)
        def _():
            @pl.loop(0, blocks)
            def _(j):
                panel_arrived(1, j)

    def products(first_row, count):
        wanted = pl.ds(pl.multiple_of(first_row, count), count)
        return jnp.dot(dense[0, wanted, :], panels[0], preferred_element_type=F32) + jnp.dot(
            dense[1, wanted, :], panels[1], preferred_element_type=F32
        )

    half = rows // 2
    pair_out[...] = products((1 - core) * half, half).astype(BF16)
    pair_copy = remote(pair_out, pair_in, rep_send.at[0], rep_recv.at[0], sibling)
    pair_copy.start()
    terms[0, pl.ds(0, half), :] = products(core * half, half)
    pair_copy.wait_recv()
    other_chip, this_chip = chunk(1 - x_hi), chunk(x_hi)
    chip_out[...] = (terms[0, other_chip, :] + pair_in[other_chip, :].astype(F32)).astype(BF16)
    chip_copy = remote(chip_out, chip_in, rep_send.at[1], rep_recv.at[1], across)
    chip_copy.start()
    partial = terms[0, this_chip, :] + pair_in[this_chip, :].astype(F32)
    chip_copy.wait_recv()
    aggregate = ((partial + chip_in[...].astype(F32)) / root).astype(BF16)

    preact = pre_self + jnp.dot(aggregate, w_neigh[...], preferred_element_type=F32)
    sigmoid_pre = jax.nn.sigmoid(preact)
    slope = sigmoid_pre * (1.0 + preact * (1.0 - sigmoid_pre))
    grad_pre = (cot[...].astype(F32) * slope).astype(BF16)
    last = (((1,), (1,)), ((), ()))
    back_proj = (lax.dot_general(grad_pre, w_neigh[...], last, preferred_element_type=F32) / root).astype(BF16)

    def place(rep):
        return chunk((rep % 2) * 2 + rep // 2)

    back[place(r), :] = back_proj
    to_across = remote(back.at[place(r)], back.at[place(r)], back_send.at[0], back_recv.at[0], across)
    to_across.start()
    to_sibling = remote(back.at[place(r)], back.at[place(r)], back_send.at[1], back_recv.at[1], sibling)
    to_sibling.start()

    outer = (((0,), (0,)), ((), ()))
    is_first_core = core == 0
    given = jnp.where(is_first_core, aggregate, own_rows)
    kept = jnp.where(is_first_core, own_rows, aggregate)
    wpair_out[...] = lax.dot_general(given, grad_pre, outer, preferred_element_type=F32).astype(BF16)
    wpair_copy = remote(wpair_out, wpair_in, wpair_sem.at[0], wpair_sem.at[1], sibling)
    wpair_copy.start()
    hidden[...] = (preact * sigmoid_pre).astype(BF16)
    weight_sum = lax.dot_general(kept, grad_pre, outer, preferred_element_type=F32)
    own_term = lax.dot_general(grad_pre, w_self[...], last, preferred_element_type=F32)

    wpair_copy.wait_recv()
    terms[1, pl.ds(0, depth), :] = weight_sum + wpair_in[...].astype(F32)
    wy_out[...] = terms[1, pl.ds(0, depth), :].astype(BF16)
    y_rows = depth // Y
    x_rows = y_rows // X

    def wy_copy(step):
        return remote(
            wy_out.at[chunk((y + step) % Y, y_rows)], wy_in.at[step - 1],
            wy_send.at[step - 1], wy_recv.at[step - 1], y_peer(step),
        )

    for step in range(1, Y):
        wy_copy(step).start()
    y_sum = terms[1, chunk(y, y_rows), :]

    to_across.wait_recv()
    passed = place((r + 2) % 4)
    passed_on = remote(back.at[passed], back.at[passed], back_send.at[2], back_recv.at[2], sibling)
    passed_on.start()
    to_sibling.wait_recv()
    passed_on.wait_recv()

    slot_a = jnp.where((r == 0) | (r == 2), 1, 0)
    slot_b = 1 - slot_a
    starts = (r == 0) | (r == 3)
    ends = (r == 1) | (r == 2)

    def compute_terms(slot):
        terms[slot] = jnp.dot(dense_t[slot], back[...], preferred_element_type=F32)

    def start_send(j):
        return remote(
            chain_out.at[slot_b, chunk(j)], chain_in.at[slot_a, chunk(j)],
            chain_send.at[slot_b, j], chain_recv.at[slot_a, j], (b_down, r),
        )

    def chain_send_a(j):
        return remote(
            chain_out.at[slot_a, chunk(j)], chain_in.at[slot_b, chunk(j)],
            chain_send.at[slot_a, j], chain_recv.at[slot_b, j], (b_down, 1 + x_hi),
        )

    def final_send_up(j):
        return remote(
            chain_out.at[slot_b, chunk(j)], final_in.at[0], chain_send.at[slot_b, j], final_recv.at[0], (b_down, j)
        )

    def final_send_here(j):
        return remote(
            chain_out.at[slot_b, chunk(j)], final_in.at[1], chain_send.at[slot_b, j], final_recv.at[1], (b, j)
        )

    def chain_arrived(slot, j):
        arrived(chain_in.at[slot, chunk(j)], chain_send.at[slot, j], chain_recv.at[slot, j])

    def summed_chunk(slot, j):
        chain_out[slot, chunk(j), :] = (
            terms[slot, chunk(j), :] + chain_in[slot, chunk(j), :].astype(F32)
        ).astype(BF16)

    compute_terms(slot_b)

    @pl.when(starts)
    def _():
        @pl.loop(0, blocks)
        def _(j):
            chain_out[slot_b, chunk(j), :] = terms[slot_b, chunk(j), :].astype(BF16)
            start_send(j).start()

    compute_terms(slot_a)

    def chain_step_a(j):
        chain_arrived(slot_a, j)
        summed_chunk(slot_a, j)
        chain_send_a(j).start()

    def chain_step_b(j):
        @pl.when(ends)
        def _():
            chain_arrived(slot_b, j)
            summed_chunk(slot_b, j)

        @pl.when(r == 1)
        def _():
            final_send_up(j).start()

        @pl.when((r == 2) & (j != 2))
        def _():
            final_send_here(j).start()

    for step in range(1, Y):
        arrived(wy_in.at[step - 1], wy_send.at[step - 1], wy_recv.at[step - 1])
        y_sum += wy_in[step - 1].astype(F32)
    wx_out[...] = y_sum.astype(BF16)

    def wx_copy(step):
        return remote(
            wx_out.at[chunk((x + step) % X, x_rows)], wx_in.at[step - 1],
            wx_send.at[step - 1], wx_recv.at[step - 1], x_peer(step),
        )

    for step in range(1, X):
        wx_copy(step).start()

    for j in range(0, 2):
        chain_step_a(j)

    x_sum = wx_out[chunk(x, x_rows), :].astype(F32)
    for step in range(1, X):
        arrived(wx_in.at[step - 1], wx_send.at[step - 1], wx_recv.at[step - 1])
        x_sum += wx_in[step - 1].astype(F32)
    wz_all[z] = x_sum.astype(BF16)

    def wz_copy(step):
        return remote(wz_all.at[z], wz_all.at[z], wz_send.at[step - 1], wz_recv.at[step - 1], z_peer(step))

    for step in range(1, Z):
        wz_copy(step).start()

    for j in range(2, blocks):
        chain_step_a(j)
    for j in range(0, 2):
        chain_step_b(j)

    for step in range(1, Z):
        source = (z + Z - step) % Z
        arrived(wz_all.at[source], wz_send.at[step - 1], wz_recv.at[step - 1])
    z_sum = wz_all[0].astype(F32)
    for index in range(1, Z):
        z_sum += wz_all[index].astype(F32)
    mine = chunk((core * Y + y) * X + x, x_rows)
    wgrad[mine, :] = z_sum.astype(BF16)

    def ax_copy(step):
        return remote(wgrad.at[mine], wgrad.at[mine], ax_send.at[step - 1], ax_recv.at[step - 1], x_peer(step))

    for step in range(1, X):
        ax_copy(step).start()

    for j in range(2, blocks):
        chain_step_b(j)

    for step in range(1, X):
        theirs = chunk((core * Y + y) * X + (x + X - step) % X, x_rows)
        arrived(wgrad.at[theirs], ax_send.at[step - 1], ax_recv.at[step - 1])
    my_y = chunk(core * Y + y, y_rows)

    def ay_copy(step):
        return remote(wgrad.at[my_y], wgrad.at[my_y], ay_send.at[step - 1], ay_recv.at[step - 1], y_peer(step))

    for step in range(1, Y):
        ay_copy(step).start()

    arrived(final_in.at[0], chain_send.at[0, 0], final_recv.at[0])

    @pl.when(r == 2)
    def _():
        final_in[1] = chain_out[0, chunk(2), :]

    @pl.when(r != 2)
    def _():
        arrived(final_in.at[1], chain_send.at[0, 0], final_recv.at[1])

    grad_feat[...] = (own_term + final_in[0].astype(F32) + final_in[1].astype(F32)).astype(BF16)

    for step in range(1, Y):
        theirs = chunk(core * Y + (y + Y - step) % Y, y_rows)
        arrived(wgrad.at[theirs], ay_send.at[step - 1], ay_recv.at[step - 1])
    my_half = chunk(core, depth)
    half_copy = remote(wgrad.at[my_half], wgrad.at[my_half], ac_sem.at[0], ac_sem.at[1], sibling)
    half_copy.start()

    @pl.when(first)
    def _():
        @pl.loop(0, blocks)
        def _(j):
            first_send(j).wait_send()

    @pl.loop(0, blocks)
    def _(j):
        relay_a(j).wait_send()
        chain_send_a(j).wait_send()

        @pl.when(r == 1)
        def _():
            relay_b(j).wait_send()
            final_send_up(j).wait_send()

        @pl.when((r == 2) & (j != 2))
        def _():
            final_send_here(j).wait_send()

        @pl.when(starts)
        def _():
            start_send(j).wait_send()

    pair_copy.wait_send()
    chip_copy.wait_send()
    to_across.wait_send()
    to_sibling.wait_send()
    passed_on.wait_send()
    wpair_copy.wait_send()
    for step in range(1, Y):
        wy_copy(step).wait_send()
        ay_copy(step).wait_send()
    for step in range(1, X):
        wx_copy(step).wait_send()
        ax_copy(step).wait_send()
    for step in range(1, Z):
        wz_copy(step).wait_send()

    scale = 1.0 / math.sqrt(rows * blk_total)
    arrived(wgrad.at[chunk(1 - core, depth)], ac_sem.at[0], ac_sem.at[1])
    grad_self[...] = wgrad[pl.ds(0, depth), :].astype(F32) * scale
    grad_neigh[...] = wgrad[pl.ds(depth, depth), :].astype(F32) * scale
    half_copy.wait_send()


def on_device(tile_vals, tile_coords, tile_live, features, degree, w_self, w_neigh, cotangent):
    tile_count, tile = tile_vals.shape[2:4]
    rows, depth = features.shape
    share = cotangent.shape[0]
    blocks = rows // tile
    half = rows // 2
    y_rows = depth // Y
    x_rows = y_rows // X
    any_space = pl.BlockSpec(memory_space=pl.ANY)
    smem = pl.BlockSpec(memory_space=pltpu.SMEM)
    vmem = pl.BlockSpec(memory_space=pltpu.VMEM)
    dma = pltpu.SemaphoreType.DMA
    return pl.pallas_call(
        layer_kernel,
        out_shape=(
            jax.ShapeDtypeStruct((share, depth), BF16),
            jax.ShapeDtypeStruct((share, depth), BF16),
            jax.ShapeDtypeStruct((depth, depth), F32),
            jax.ShapeDtypeStruct((depth, depth), F32),
        ),
        in_specs=[any_space, smem, smem, any_space, vmem, vmem, vmem, vmem],
        out_specs=(vmem, vmem, vmem, vmem),
        scratch_shapes=[
            pltpu.VMEM((2, tile_count, tile, tile), BF16),
            pltpu.VMEM((share, depth), BF16),
            pltpu.VMEM((2, rows, depth), BF16),
            pltpu.VMEM((2, rows, rows), BF16),
            pltpu.VMEM((2, rows, rows), BF16),
            pltpu.VMEM((half, depth), BF16),
            pltpu.VMEM((half, depth), BF16),
            pltpu.VMEM((share, depth), BF16),
            pltpu.VMEM((share, depth), BF16),
            pltpu.VMEM((rows, depth), BF16),
            pltpu.VMEM((depth, depth), BF16),
            pltpu.VMEM((depth, depth), BF16),
            pltpu.VMEM((depth, depth), BF16),
            pltpu.VMEM((Y - 1, y_rows, depth), BF16),
            pltpu.VMEM((y_rows, depth), BF16),
            pltpu.VMEM((X - 1, x_rows, depth), BF16),
            pltpu.VMEM((Z, x_rows, depth), BF16),
            pltpu.VMEM((2 * depth, depth), BF16),
            pltpu.VMEM((2, rows, depth), F32),
            pltpu.VMEM((2, rows, depth), BF16),
            pltpu.VMEM((2, rows, depth), BF16),
            pltpu.VMEM((2, share, depth), BF16),
            dma((3,)),
            dma((blocks,)),
            dma((2, blocks)),
            dma((2, blocks)),
            dma((2,)),
            dma((2,)),
            dma((3,)),
            dma((3,)),
            dma((2,)),
            dma((Y - 1,)),
            dma((Y - 1,)),
            dma((X - 1,)),
            dma((X - 1,)),
            dma((Z - 1,)),
            dma((Z - 1,)),
            dma((X - 1,)),
            dma((X - 1,)),
            dma((Y - 1,)),
            dma((Y - 1,)),
            dma((2,)),
            dma((2, blocks)),
            dma((2, blocks)),
            dma((2,)),
        ],
        compiler_params=pltpu.CompilerParams(collective_id=0, has_side_effects=True),
    )(
        tile_vals, tile_coords, tile_live, features,
        degree.reshape(1, share), w_self, w_neigh, cotangent,
    )


def solution(mesh):
    return jax.shard_map(
        on_device,
        mesh=mesh,
        in_specs=(
            P("blk", "rep", None, None, None),
            P("blk", "rep", None, None),
            P("blk", "rep", None),
            P("blk", None),
            P(("blk", "rep")),
            P(),
            P(),
            P(("blk", "rep"), None),
        ),
        out_specs=(P(("blk", "rep"), None), P(("blk", "rep"), None), P(), P()),
        check_vma=False,
    )
```

```python
import functools
import functools
import math

import jax
import jax.numpy as jnp
from jax import lax
from jax.experimental import pallas as pl
from jax.experimental.pallas import tpu as pltpu
from jax.sharding import PartitionSpec as P

Y, X_LO, Z, X_HI = 4, 2, 8, 2
X = X_LO * X_HI
PLANE = X * Y
MESH = pl.DeviceIdType.MESH
F32, BF16 = jnp.float32, jnp.bfloat16


def flag(cond):
    return jnp.where(cond, 1, 0)


def layer_kernel(
    tiles_hbm, coords_hbm, live_hbm, feat_hbm, degree_hbm, w_self_hbm, w_neigh_hbm, cot_hbm,
    hidden, grad_feat, wgrad,
    coords, live, degree, w_self, w_neigh, cot,
    tiles, own, panels, dense, dense_t, pair_out, pair_in, chip_out, chip_in, back,
    wpair_out, wpair_in, plane_out, plane_in, z_all,
    terms, chain_out, chain_in, final_in,
    local_sem, feat_send, relay_send, feat_recv, rep_send, rep_recv, back_send, back_recv,
    wpair_sem, plane_send, plane_recv, z_send, z_recv, share_send, share_recv, half_sem,
    chain_send, chain_recv, final_recv,
):
    blk_total = Y * X_LO * Z
    b, r = lax.axis_index("blk"), lax.axis_index("rep")
    z, x_lo, y = b % Z, (b // Z) % X_LO, b // (Z * X_LO)
    x_hi, core = r // 2, r % 2
    x = x_hi * X_LO + x_lo
    tile = tiles.shape[2]
    depth = own.shape[1]
    rows = panels.shape[1]
    blocks = rows // tile
    tile_count = tiles.shape[1]
    up = jnp.where(x_hi == 0, 1, blk_total - 1)
    b_up = (b + up) % blk_total
    b_down = (b + blk_total - up) % blk_total

    def plane_place(step):
        return ((y + step // X) % Y) * X + (x + step) % X

    def plane_source(step):
        return ((y + Y - step // X) % Y) * X + (x + X - step % X) % X

    def plane_peer(step):
        at_x = (x + step) % X
        return (((y + step // X) % Y) * X_LO + at_x % X_LO) * Z + z, (at_x // X_LO) * 2 + core

    def z_peer(step):
        return (y * X_LO + x_lo) * Z + (z + step) % Z, r

    sibling = (b, r + 1 - 2 * core)
    across = (b, (r + 2) % 4)

    def remote(src, dst, send, recv, peer):
        return pltpu.make_async_remote_copy(
            src_ref=src, dst_ref=dst, send_sem=send, recv_sem=recv, device_id=peer, device_id_type=MESH
        )

    def arrived(dst, send, recv):
        remote(dst, dst, send, recv, sibling).wait_recv()

    def chunk(index, size=tile):
        return pl.ds(pl.multiple_of(index * size, size), size)

    staged = [
        (coords_hbm, coords), (live_hbm, live), (tiles_hbm.at[0], tiles), (feat_hbm.at[chunk(r)], own),
        (degree_hbm, degree), (w_self_hbm, w_self), (w_neigh_hbm, w_neigh), (cot_hbm, cot),
    ]
    staging = [
        pltpu.make_async_copy(src, dst, local_sem.at[index + 1]) for index, (src, dst) in enumerate(staged)
    ]

    panel_copy = pltpu.make_async_copy(feat_hbm, panels.at[0], local_sem.at[0])

    barrier = pltpu.get_barrier_semaphore()
    greeted = 0
    peers = [(b_next, (r + turn) % 4) for b_next in (b_up, b_down) for turn in range(4)]
    peers += [(b, (r + turn) % 4) for turn in range(1, 4)]
    peers += [plane_peer(step) for step in range(1, PLANE)]
    peers += [z_peer(step) for step in range(1, Z)]
    for peer in peers:
        pl.semaphore_signal(barrier, inc=1, device_id=peer, device_id_type=MESH)
        greeted += 1
    for copy in staging:
        copy.start()

    @pl.when(r == 2)
    def _():
        panel_copy.start()

    pl.semaphore_wait(barrier, greeted)

    first = (r == 1) | (r == 2)
    relay_slot = jnp.where(r == 3, 0, 1)
    relay_rep = jnp.where(r == 2, 3, r)

    def first_send(j):
        return remote(
            feat_hbm.at[chunk(j)], panels.at[1, chunk(j)], feat_send.at[j], feat_recv.at[1, j], (b_up, r)
        )

    def relay_a(j):
        return remote(
            panels.at[relay_slot, chunk(j)], panels.at[1 - relay_slot, chunk(j)],
            relay_send.at[0, j], feat_recv.at[1 - relay_slot, j], (b_up, relay_rep),
        )

    def relay_b(j):
        return remote(
            panels.at[0, chunk(j)], panels.at[1, chunk(j)], relay_send.at[1, j], feat_recv.at[1, j], (b_up, 0)
        )

    def panel_arrived(slot, j):
        arrived(panels.at[slot, chunk(j)], feat_send.at[j], feat_recv.at[slot, j])

    @pl.when(first)
    def _():
        @pl.loop(0, blocks)
        def _(j):
            first_send(j).start()

    for copy in staging:
        copy.wait()

    def build(slot, i):
        at = (i % 2) * 2 + i // 2

        @pl.loop(0, blocks)
        def _(j):
            total = jnp.zeros((tile, tile), F32)
            for k in range(tile_count):
                here = (coords[0, slot, 0, k] == i) & (coords[0, slot, 1, k] == j)
                weight = (flag(here) * live[0, slot, k]).astype(F32)
                total += tiles[slot, k].astype(F32) * weight
            dense[slot, chunk(at), chunk(j)] = total.astype(BF16)
            dense_t[slot, chunk(j), chunk(at)] = total.T.astype(BF16)

    @pl.loop(0, blocks)
    def _(j):
        build(0, j)
        panel_arrived(relay_slot, j)
        relay_a(j).start()

    @pl.loop(0, blocks)
    def _(j):
        build(1, j)

        @pl.when(r == 1)
        def _():
            panel_arrived(0, j)
            relay_b(j).start()

    own_rows = own[...]
    pre_self = jnp.dot(own_rows, w_self[...], preferred_element_type=F32)
    degrees = jnp.broadcast_to(degree[...].astype(F32), (tile, tile))
    root_half = jnp.sqrt(degrees.T)
    root = jnp.concatenate([root_half] * (depth // tile), axis=1)

    @pl.when(r == 2)
    def _():
        panel_copy.wait()

    @pl.when(r == 0)
    def _():
        @pl.loop(0, blocks)
        def _(j):
            panel_arrived(0, j)

    @pl.when((r == 2) | (r == 3))
    def _():
        @pl.when(r == 3)
        def _():
            @pl.loop(0, blocks)
            def _(j):
                panel_arrived(1, j)

    def panels_left():
        @pl.when(first)
        def _():
            @pl.loop(0, blocks)
            def _(j):
                first_send(j).wait_send()

        @pl.loop(0, blocks)
        def _(j):
            relay_a(j).wait_send()

            @pl.when(r == 1)
            def _():
                relay_b(j).wait_send()

    def products(first_row, count):
        wanted = pl.ds(pl.multiple_of(first_row, count), count)
        return jnp.dot(dense[0, wanted, :], panels[0], preferred_element_type=F32) + jnp.dot(
            dense[1, wanted, :], panels[1], preferred_element_type=F32
        )

    half = rows // 2
    pair_out[...] = products((1 - core) * half, half).astype(BF16)
    pair_copy = remote(pair_out, pair_in, rep_send.at[0], rep_recv.at[0], sibling)
    pair_copy.start()
    terms[0, pl.ds(0, half), :] = products(core * half, half)
    pair_copy.wait_recv()
    other_chip, this_chip = chunk(1 - x_hi), chunk(x_hi)
    chip_out[...] = (terms[0, other_chip, :] + pair_in[other_chip, :].astype(F32)).astype(BF16)
    chip_copy = remote(chip_out, chip_in, rep_send.at[1], rep_recv.at[1], across)
    chip_copy.start()
    partial = terms[0, this_chip, :] + pair_in[this_chip, :].astype(F32)
    chip_copy.wait_recv()
    aggregate = ((partial + chip_in[...].astype(F32)) / root).astype(BF16)

    def sums_left():
        pair_copy.wait_send()
        chip_copy.wait_send()

    preact = pre_self + jnp.dot(aggregate, w_neigh[...], preferred_element_type=F32)
    sigmoid_pre = jax.nn.sigmoid(preact)
    slope = sigmoid_pre * (1.0 + preact * (1.0 - sigmoid_pre))
    grad_pre = (cot[...].astype(F32) * slope).astype(BF16)
    last = (((1,), (1,)), ((), ()))
    back_proj = (lax.dot_general(grad_pre, w_neigh[...], last, preferred_element_type=F32) / root).astype(BF16)

    def place(rep):
        return chunk((rep % 2) * 2 + rep // 2)

    back[place(r), :] = back_proj
    to_across = remote(back.at[place(r)], back.at[place(r)], back_send.at[0], back_recv.at[0], across)
    to_across.start()
    to_sibling = remote(back.at[place(r)], back.at[place(r)], back_send.at[1], back_recv.at[1], sibling)
    to_sibling.start()

    outer = (((0,), (0,)), ((), ()))
    is_first_core = core == 0
    given = jnp.where(is_first_core, aggregate, own_rows)
    kept = jnp.where(is_first_core, own_rows, aggregate)
    wpair_out[...] = lax.dot_general(given, grad_pre, outer, preferred_element_type=F32).astype(BF16)
    wpair_copy = remote(wpair_out, wpair_in, wpair_sem.at[0], wpair_sem.at[1], sibling)
    wpair_copy.start()
    hidden[...] = (preact * sigmoid_pre).astype(BF16)
    weight_sum = lax.dot_general(kept, grad_pre, outer, preferred_element_type=F32)
    own_term = lax.dot_general(grad_pre, w_self[...], last, preferred_element_type=F32)

    wpair_copy.wait_recv()
    terms[1, pl.ds(0, depth), :] = weight_sum + wpair_in[...].astype(F32)
    plane_out[...] = terms[1, pl.ds(0, depth), :].astype(BF16)
    share_rows = depth // PLANE

    def plane_copy(step):
        return remote(
            plane_out.at[chunk(plane_place(step), share_rows)], plane_in.at[step - 1],
            plane_send.at[step - 1], plane_recv.at[step - 1], plane_peer(step),
        )

    @pl.loop(1, PLANE)
    def _(step):
        plane_copy(step).start()

    place_here = y * X + x
    plane_sum = terms[1, chunk(place_here, share_rows), :]

    to_across.wait_recv()
    passed = place((r + 2) % 4)
    passed_on = remote(back.at[passed], back.at[passed], back_send.at[2], back_recv.at[2], sibling)
    passed_on.start()
    to_sibling.wait_recv()
    passed_on.wait_recv()

    def back_left():
        to_across.wait_send()
        to_sibling.wait_send()
        passed_on.wait_send()

    slot_a = jnp.where((r == 0) | (r == 2), 1, 0)
    slot_b = 1 - slot_a
    starts = (r == 0) | (r == 3)
    ends = (r == 1) | (r == 2)

    def compute_terms(slot):
        terms[slot] = jnp.dot(dense_t[slot], back[...], preferred_element_type=F32)

    def start_send(j):
        return remote(
            chain_out.at[slot_b, chunk(j)], chain_in.at[slot_a, chunk(j)],
            chain_send.at[slot_b, j], chain_recv.at[slot_a, j], (b_down, r),
        )

    def chain_send_a(j):
        return remote(
            chain_out.at[slot_a, chunk(j)], chain_in.at[slot_b, chunk(j)],
            chain_send.at[slot_a, j], chain_recv.at[slot_b, j], (b_down, 1 + x_hi),
        )

    def final_send_up(j):
        return remote(
            chain_out.at[slot_b, chunk(j)], final_in.at[0], chain_send.at[slot_b, j], final_recv.at[0], (b_down, j)
        )

    def final_send_here(j):
        return remote(
            chain_out.at[slot_b, chunk(j)], final_in.at[1], chain_send.at[slot_b, j], final_recv.at[1], (b, j)
        )

    def chain_arrived(slot, j):
        arrived(chain_in.at[slot, chunk(j)], chain_send.at[slot, j], chain_recv.at[slot, j])

    def summed_chunk(slot, j):
        chain_out[slot, chunk(j), :] = (
            terms[slot, chunk(j), :] + chain_in[slot, chunk(j), :].astype(F32)
        ).astype(BF16)

    compute_terms(slot_b)

    @pl.when(starts)
    def _():
        @pl.loop(0, blocks)
        def _(j):
            chain_out[slot_b, chunk(j), :] = terms[slot_b, chunk(j), :].astype(BF16)
            start_send(j).start()

    compute_terms(slot_a)

    def chain_step_a(j):
        chain_arrived(slot_a, j)
        summed_chunk(slot_a, j)
        chain_send_a(j).start()

    def chain_step_b(j):
        @pl.when(ends)
        def _():
            chain_arrived(slot_b, j)
            summed_chunk(slot_b, j)

        @pl.when(r == 1)
        def _():
            final_send_up(j).start()

        @pl.when((r == 2) & (j != 2))
        def _():
            final_send_here(j).start()

    def chain_left():
        @pl.loop(0, blocks)
        def _(j):
            chain_send_a(j).wait_send()

            @pl.when(r == 1)
            def _():
                final_send_up(j).wait_send()

            @pl.when((r == 2) & (j != 2))
            def _():
                final_send_here(j).wait_send()

            @pl.when(starts)
            def _():
                start_send(j).wait_send()

    for step in range(1, PLANE):
        arrived(plane_in.at[step - 1], plane_send.at[step - 1], plane_recv.at[step - 1])
        plane_sum += plane_in[step - 1].astype(F32)
    z_all[z] = plane_sum.astype(BF16)

    def z_copy(step):
        return remote(z_all.at[z], z_all.at[z], z_send.at[step - 1], z_recv.at[step - 1], z_peer(step))

    for step in range(1, Z):
        z_copy(step).start()

    @pl.when(starts)
    def _():
        @pl.loop(0, blocks)
        def _(j):
            chain_step_a(j)

    for step in range(1, Z):
        arrived(z_all.at[(z + Z - step) % Z], z_send.at[step - 1], z_recv.at[step - 1])
    z_sum = z_all[0].astype(F32)
    for index in range(1, Z):
        z_sum += z_all[index].astype(F32)

    def share_at(place):
        return chunk(core * PLANE + place, share_rows)

    wgrad[share_at(place_here), :] = z_sum.astype(BF16)

    def share_copy(step):
        mine = share_at(place_here)
        return remote(
            wgrad.at[mine], wgrad.at[mine], share_send.at[step - 1], share_recv.at[step - 1], plane_peer(step)
        )

    @pl.loop(1, PLANE)
    def _(step):
        share_copy(step).start()

    @pl.when(ends)
    def _():
        @pl.loop(0, blocks)
        def _(j):
            chain_step_a(j)

    @pl.loop(0, blocks)
    def _(j):
        chain_step_b(j)

    arrived(final_in.at[0], chain_send.at[0, 0], final_recv.at[0])

    @pl.when(r == 2)
    def _():
        final_in[1] = chain_out[0, chunk(2), :]

    @pl.when(r != 2)
    def _():
        arrived(final_in.at[1], chain_send.at[0, 0], final_recv.at[1])

    grad_feat[...] = (own_term + final_in[0].astype(F32) + final_in[1].astype(F32)).astype(BF16)

    @pl.loop(1, PLANE)
    def _(step):
        arrived(wgrad.at[share_at(plane_source(step))], share_send.at[step - 1], share_recv.at[step - 1])

    my_half = chunk(core, depth)
    half_copy = remote(wgrad.at[my_half], wgrad.at[my_half], half_sem.at[0], half_sem.at[1], sibling)
    half_copy.start()

    def weights_left():
        wpair_copy.wait_send()

        @pl.loop(1, PLANE)
        def _(step):
            plane_copy(step).wait_send()
            share_copy(step).wait_send()

        for step in range(1, Z):
            z_copy(step).wait_send()

    panels_left()
    sums_left()
    back_left()
    chain_left()
    weights_left()
    arrived(wgrad.at[chunk(1 - core, depth)], half_sem.at[0], half_sem.at[1])
    half_copy.wait_send()


def result_kernel(hidden, grad_feat, wgrad, hidden_out, grad_feat_out, grad_self, grad_neigh, *, scale):
    hidden_out[...] = hidden[...]
    grad_feat_out[...] = grad_feat[...]
    depth = grad_self.shape[0]
    grad_self[...] = wgrad[pl.ds(0, depth), :].astype(F32) * scale
    grad_neigh[...] = wgrad[pl.ds(depth, depth), :].astype(F32) * scale


def on_device(tile_vals, tile_coords, tile_live, features, degree, w_self, w_neigh, cotangent):
    tile_count, tile = tile_vals.shape[2:4]
    rows, depth = features.shape
    share = cotangent.shape[0]
    blocks = rows // tile
    half = rows // 2
    share_rows = depth // PLANE
    any_space = pl.BlockSpec(memory_space=pl.ANY)
    vmem = pl.BlockSpec(memory_space=pltpu.VMEM)
    dma = pltpu.SemaphoreType.DMA
    nodes = jax.ShapeDtypeStruct((share, depth), BF16)
    weights = jax.ShapeDtypeStruct((depth, depth), F32)
    hidden, grad_feat, wgrad = pl.pallas_call(
        layer_kernel,
        out_shape=(nodes, nodes, jax.ShapeDtypeStruct((2 * depth, depth), BF16)),
        in_specs=[any_space] * 8,
        out_specs=(vmem, vmem, vmem),
        scratch_shapes=[
            pltpu.SMEM((1, 2, 2, tile_count), jnp.int32),
            pltpu.SMEM((1, 2, tile_count), jnp.int32),
            pltpu.VMEM((1, share), jnp.int32),
            pltpu.VMEM((depth, depth), BF16),
            pltpu.VMEM((depth, depth), BF16),
            pltpu.VMEM((share, depth), BF16),
            pltpu.VMEM((2, tile_count, tile, tile), BF16),
            pltpu.VMEM((share, depth), BF16),
            pltpu.VMEM((2, rows, depth), BF16),
            pltpu.VMEM((2, rows, rows), BF16),
            pltpu.VMEM((2, rows, rows), BF16),
            pltpu.VMEM((half, depth), BF16),
            pltpu.VMEM((half, depth), BF16),
            pltpu.VMEM((share, depth), BF16),
            pltpu.VMEM((share, depth), BF16),
            pltpu.VMEM((rows, depth), BF16),
            pltpu.VMEM((depth, depth), BF16),
            pltpu.VMEM((depth, depth), BF16),
            pltpu.VMEM((depth, depth), BF16),
            pltpu.VMEM((PLANE - 1, share_rows, depth), BF16),
            pltpu.VMEM((Z, share_rows, depth), BF16),
            pltpu.VMEM((2, rows, depth), F32),
            pltpu.VMEM((2, rows, depth), BF16),
            pltpu.VMEM((2, rows, depth), BF16),
            pltpu.VMEM((2, share, depth), BF16),
            dma((9,)),
            dma((blocks,)),
            dma((2, blocks)),
            dma((2, blocks)),
            dma((2,)),
            dma((2,)),
            dma((3,)),
            dma((3,)),
            dma((2,)),
            dma((PLANE - 1,)),
            dma((PLANE - 1,)),
            dma((Z - 1,)),
            dma((Z - 1,)),
            dma((PLANE - 1,)),
            dma((PLANE - 1,)),
            dma((2,)),
            dma((2, blocks)),
            dma((2, blocks)),
            dma((2,)),
        ],
        compiler_params=pltpu.CompilerParams(collective_id=0, has_side_effects=True),
    )(
        tile_vals, jnp.swapaxes(tile_coords, 2, 3), tile_live, features,
        degree.reshape(1, share), w_self, w_neigh, cotangent,
    )
    scale = 1.0 / math.sqrt(rows * lax.axis_size("blk"))
    return pl.pallas_call(
        functools.partial(result_kernel, scale=scale),
        out_shape=(nodes, nodes, weights, weights),
        in_specs=[vmem, vmem, vmem],
        out_specs=(vmem, vmem, vmem, vmem),
    )(hidden, grad_feat, wgrad)


def solution(mesh):
    return jax.shard_map(
        on_device,
        mesh=mesh,
        in_specs=(
            P("blk", "rep", None, None, None),
            P("blk", "rep", None, None),
            P("blk", "rep", None),
            P("blk", None),
            P(("blk", "rep")),
            P(),
            P(),
            P(("blk", "rep"), None),
        ),
        out_specs=(P(("blk", "rep"), None), P(("blk", "rep"), None), P(), P()),
        check_vma=False,
    )
```
